256 devices in a mesh: head: 8 (over y, core), ctx: 32 (over z, x).
Axes of the slice: x: 4, y: 4, z: 8, core: 2. Of those that a mesh axis runs over, the one named last changes fastest.
Arguments:
- queries: bfloat16 [24576, 8192], P(('ctx', 'head')), may hold values from -6 to 6
- keys: bfloat16 [24576, 8192], P(('ctx', 'head')), may hold values from -6 to 6
- values: bfloat16 [24576, 8192], P(('ctx', 'head')), may hold values from -6 to 6
- pattern: int32 [3, 32, 6, 6], P(None, 'ctx'), may hold values 0 or 1
Outputs:
- attended: bfloat16 [24576, 8192], P(('ctx', 'head'))
The draws below stay inside these ranges and needn't reach their ends.
All inputs are finite; a program needn't handle non-finite values. No bound on the sum of `pattern` on one device may be relied on, other than what follows from the above.
Results may differ from the reference program's by a relative error of at most 0.009.
Values may be sent and summed in bfloat16 or wider, within the bound.
No kernel may reach another device: no remote copies, remote signals or barrier semaphores. Data moves between devices by JAX's collectives and lax.ppermute only.
A program may use at most 128 MiB of HBM per device.

```python
import jax
import jax.numpy as jnp
from jax import lax

H = 64
HD = 128
BLOCK = 128
C = 768
QB = 6
WIDTH = 8192
TOKENS = 24576
N_CTX = 32


def query_key_pair(key):
    base = jax.random.fold_in(key, 7)
    first_key, second_key = jax.random.split(base, 2)
    shape = (TOKENS, H * HD)
    query_draw = jnp.clip(jax.random.normal(first_key, shape, jnp.float32), -6.0, 6.0)
    key_draw = jnp.clip(jax.random.normal(second_key, shape, jnp.float32), -6.0, 6.0)
    return (query_draw, key_draw)


def draw_queries(key, part):
    return query_key_pair(key)[0].astype(jnp.bfloat16)


def draw_keys(key, part):
    return query_key_pair(key)[1].astype(jnp.bfloat16)


def plant(values, rng, smallest, largest):
    extent = values.shape
    spot = [jax.random.randint(jax.random.fold_in(rng, axis), (), 0, extent[axis]) for axis in range(len(extent))]
    values = values.at[tuple(spot)].set(smallest)
    longest = extent.index(max(extent))
    spot[longest] = (spot[longest] + 1) % extent[longest]
    return values.at[tuple(spot)].set(largest)


def levels(rng, shape, pieces, low, largest):
    def one(dim, parts):
        draws = jax.random.uniform(jax.random.fold_in(jax.random.fold_in(rng, 6), dim), (parts,), jnp.float32, low / len(pieces), largest / len(pieces))
        return jnp.repeat(jnp.exp(draws), shape[dim] // parts).reshape((-1,) + (1,) * (len(shape) - dim - 1))

    level = one(*pieces[0])
    for cut in pieces[1:]:
        level = level * one(*cut)
    return level


def bell_draw(stream_key, dims, spread, limit, pieces=(), kind=jnp.bfloat16):
    loudness = levels(stream_key, dims, pieces, -0.22, 0.18) if pieces else 1.0
    values = jax.random.normal(stream_key, dims, jnp.float32) * spread * loudness
    return jnp.minimum(jnp.maximum(values, -limit), limit).astype(kind)


def setup_inputs(seed: int = 0) -> dict:
    seeds = jax.random.split(jax.random.key(seed), 5)
    queries = draw_queries(jax.random.fold_in(seeds[4], 71), 0)
    keys = draw_keys(jax.random.fold_in(seeds[4], 71), 0)
    values = bell_draw(seeds[2], (TOKENS, WIDTH), 1.0, 6.0, ((0, 256),))
    pattern = plant((jax.random.randint(seeds[3], (3, N_CTX, QB, QB), 0, 2) < 1).astype(jnp.int32), jax.random.fold_in(seeds[3], 1), 0, 1)
    return {"queries": queries, "keys": keys, "values": values, "pattern": pattern}


masked_score = -1e30


def block_allow(block_flags):
    tiled = jnp.broadcast_to(block_flags[:, None, :, None], (QB, BLOCK, QB, BLOCK))
    return tiled.reshape(QB * BLOCK, QB * BLOCK) > 0


def reference(queries, keys, values, pattern):
    far = N_CTX // 2
    distances = (far - 1, far, far + 1)
    scaling = HD ** -0.5
    tok_rows = jnp.arange(C, dtype=jnp.int32)
    causal = tok_rows[:, None] >= tok_rows[None, :]

    def take_rows(array, first_row):
        return lax.dynamic_slice_in_dim(array, first_row, C, 0)

    def one_span(span):
        first_row = (span * C).astype(jnp.int32)
        key_parts = [take_rows(keys, first_row)]
        value_parts = [take_rows(values, first_row)]
        allow_parts = [causal]
        for number, distance in enumerate(distances):
            source_row = (jnp.maximum(span - distance, 0) * C).astype(jnp.int32)
            key_parts.append(take_rows(keys, source_row))
            value_parts.append(take_rows(values, source_row))
            block_flags = lax.dynamic_index_in_dim(pattern[number], span, 0, keepdims=False)
            allow_parts.append(block_allow(block_flags) & (span >= distance))
        key_all = jnp.concatenate(key_parts, 0)
        value_all = jnp.concatenate(value_parts, 0)
        allowed = jnp.concatenate(allow_parts, 1)
        span_queries = take_rows(queries, first_row)

        def one_head(head):
            column = (head * HD).astype(jnp.int32)
            head_queries = lax.dynamic_slice_in_dim(span_queries, column, HD, 1)
            head_keys = lax.dynamic_slice_in_dim(key_all, column, HD, 1)
            head_values = lax.dynamic_slice_in_dim(value_all, column, HD, 1)
            scores = jnp.dot(head_queries, head_keys.T, preferred_element_type=jnp.float32) * scaling
            scores = jnp.where(allowed, scores, masked_score)
            maxima = jnp.max(scores, axis=1, keepdims=True)
            expo = jnp.where(allowed, jnp.exp(scores - maxima), 0.0)
            weights = (expo / jnp.sum(expo, axis=1, keepdims=True)).astype(jnp.bfloat16)
            return jnp.dot(weights, head_values, preferred_element_type=jnp.float32).astype(jnp.bfloat16)

        per_head = lax.map(one_head, jnp.arange(H, dtype=jnp.int32))
        return per_head.transpose(1, 0, 2).reshape(C, H * HD)

    result = lax.map(one_span, jnp.arange(N_CTX, dtype=jnp.int32))
    return result.reshape(TOKENS, H * HD)
```

```python
import functools
import math

import jax
import jax.numpy as jnp
from jax import lax
from jax.experimental import pallas as pl
from jax.experimental.pallas import tpu as pltpu
from jax.sharding import PartitionSpec as P


H = 64
HD = 128
BLOCK = 128
C = 768
QB = C // BLOCK
CHUNKS = 4
ROWS = 256
STEPS = C // ROWS
TAIL = 24
NEG = -1e30
FACTOR = HD**-0.5 * math.log2(math.e)


def eye():
    return lax.broadcasted_iota(jnp.int32, (BLOCK, BLOCK), 0) == lax.broadcasted_iota(
        jnp.int32, (BLOCK, BLOCK), 1
    )


def dot_t(a, b):
    return lax.dot_general(a, b, (((1,), (1,)), ((), ())), preferred_element_type=jnp.float32)


def far_kernel(
    active, q_ref, ka_ref, va_ref, kb_ref, vb_ref, kc_ref, vc_ref, bias_ref, o_ref, vx_ref, lse_ref
):
    step = pl.program_id(1)

    @pl.when(active[0] > 0)
    def _():
        @pl.when(step == 0)
        def _():
            for i, v_ref in enumerate((va_ref, vb_ref, vc_ref)):
                vx_ref[i, :, :HD] = v_ref[...]
                vx_ref[i, :, HD:] = jnp.ones((C, HD), jnp.bfloat16)
            lse_ref[...] = jnp.zeros_like(lse_ref)

        q = q_ref[...]
        scores = []
        for i, k_ref in enumerate((ka_ref, kb_ref, kc_ref)):
            raw = dot_t(q, k_ref[...]) * FACTOR
            parts = [
                raw[r * BLOCK : (r + 1) * BLOCK]
                + bias_ref[pl.ds(step * (ROWS // BLOCK) + r, 1), i * C : (i + 1) * C]
                for r in range(ROWS // BLOCK)
            ]
            scores.append(jnp.concatenate(parts, 0))
        top = functools.reduce(
            jnp.maximum, [jnp.max(s, axis=1, keepdims=True) for s in scores]
        )
        total = jnp.zeros((ROWS, 2 * HD), jnp.float32)
        for i, s in enumerate(scores):
            p = jnp.exp2(s - top).astype(jnp.bfloat16)
            total = total + jnp.dot(p, vx_ref[i], preferred_element_type=jnp.float32)
        sums = total[:, HD:]
        start = pl.multiple_of(step * ROWS, ROWS)
        o_ref[pl.ds(start, ROWS), :] = (total[:, :HD] / sums).astype(jnp.bfloat16)
        lse = top + jnp.log2(sums)
        for r in range(ROWS // BLOCK):
            line = jnp.sum(
                jnp.where(eye(), lse[r * BLOCK : (r + 1) * BLOCK], 0.0), axis=0, keepdims=True
            )
            lse_ref[pl.ds(step * (ROWS // BLOCK) + r, 1), :] = line

        @pl.when(step == STEPS - 1)
        def _():
            rest = lse_ref[...]
            terms = []
            for _ in range(3):
                term = rest.astype(jnp.bfloat16).astype(jnp.float32)
                terms.append(term)
                rest = rest - term
            o_ref[C:, :] = jnp.concatenate(terms, 0).astype(jnp.bfloat16)


def pack_kernel(groups, cols, n, *refs):
    *sources, packed, sem = refs
    width = sources[0].shape[1] // groups
    copies = []
    for i, source in enumerate(sources):
        for g in range(groups):
            copies.append(
                pltpu.make_async_copy(
                    source.at[:, pl.ds(g * width + n * cols, cols)],
                    packed.at[g, :, pl.ds(i * cols, cols)],
                    sem.at[i, g],
                )
            )
    for copy in copies:
        copy.start()
    for copy in copies:
        copy.wait()


def pack(sources, groups, cols, n):
    rows = sources[0].shape[0]
    return pl.pallas_call(
        functools.partial(pack_kernel, groups, cols, n),
        out_shape=jax.ShapeDtypeStruct((groups, rows, len(sources) * cols), jnp.bfloat16),
        in_specs=[pl.BlockSpec(memory_space=pl.ANY)] * len(sources),
        out_specs=pl.BlockSpec(memory_space=pl.ANY),
        scratch_shapes=[pltpu.SemaphoreType.DMA((len(sources), groups))],
        name="pack",
    )(*sources)


def unpack_kernel(groups, cols, n, *refs):
    piece, whole, sem = refs[0], refs[-2], refs[-1]
    width = whole.shape[1] // groups
    copies = [
        pltpu.make_async_copy(
            piece.at[g], whole.at[:, pl.ds(g * width + n * cols, cols)], sem.at[g]
        )
        for g in range(groups)
    ]
    for copy in copies:
        copy.start()
    for copy in copies:
        copy.wait()


def unpack(piece, whole, width, n):
    groups, rows, cols = piece.shape
    operands = (piece,) if whole is None else (piece, whole)
    return pl.pallas_call(
        functools.partial(unpack_kernel, groups, cols, n),
        out_shape=jax.ShapeDtypeStruct((rows, width), jnp.bfloat16),
        in_specs=[pl.BlockSpec(memory_space=pl.ANY)] * len(operands),
        out_specs=pl.BlockSpec(memory_space=pl.ANY),
        scratch_shapes=[pltpu.SemaphoreType.DMA((groups,))],
        input_output_aliases={} if whole is None else {1: 0},
        name="unpack",
    )(*operands)


def far_attention(active, far_q, own, before, after, bias, heads):
    def kv(part):
        return pl.BlockSpec((C, HD), lambda h, s, *_: (0, part * heads + h))

    return pl.pallas_call(
        far_kernel,
        out_shape=jax.ShapeDtypeStruct((C + TAIL, heads * HD), jnp.bfloat16),
        grid_spec=pltpu.PrefetchScalarGridSpec(
            num_scalar_prefetch=1,
            grid=(heads, STEPS),
            in_specs=[
                pl.BlockSpec((ROWS, HD), lambda h, s, *_: (s, h)),
                kv(0), kv(1), kv(0), kv(1), kv(0), kv(1),
                pl.BlockSpec((8, 3 * C), lambda h, s, *_: (0, 0)),
            ],
            out_specs=pl.BlockSpec((C + TAIL, HD), lambda h, s, *_: (0, h)),
            scratch_shapes=[
                pltpu.VMEM((3, C, 2 * HD), jnp.bfloat16),
                pltpu.VMEM((8, BLOCK), jnp.float32),
            ],
        ),
        name="far_attention",
    )(active, far_q, after, after, own, own, before, before, bias)


def near_kernel(receives, q_ref, k_ref, v_ref, far_ref, o_ref, vx_ref):
    vx_ref[:, :HD] = v_ref[...]
    vx_ref[:, HD:] = jnp.ones((C, HD), jnp.bfloat16)
    tail = far_ref[C:, :].astype(jnp.float32)
    lse_all = tail[0:8] + (tail[8:16] + tail[16:24])
    lse_all = jnp.where(receives[0] > 0, lse_all, NEG)
    for step in range(STEPS):
        lo, hi = step * ROWS, (step + 1) * ROWS
        s = dot_t(q_ref[lo:hi, :], k_ref[:hi, :]) * FACTOR
        rows = lo + lax.broadcasted_iota(jnp.int32, (ROWS, hi), 0)
        cols = lax.broadcasted_iota(jnp.int32, (ROWS, hi), 1)
        s = jnp.where(rows >= cols, s, NEG)
        top = jnp.max(s, axis=1, keepdims=True)
        p = jnp.exp2(s - top).astype(jnp.bfloat16)
        total = jnp.dot(p, vx_ref[:hi, :], preferred_element_type=jnp.float32)
        columns = []
        for r in range(ROWS // BLOCK):
            line = lse_all[step * (ROWS // BLOCK) + r][None, :]
            columns.append(jnp.sum(jnp.where(eye(), line, 0.0), axis=1, keepdims=True))
        far_lse = jnp.concatenate(columns, 0)
        peak = jnp.maximum(top, far_lse)
        near_w = jnp.exp2(top - peak)
        far_w = jnp.exp2(far_lse - peak)
        far_o = far_ref[lo:hi, :].astype(jnp.float32)
        upper = total[:, :HD] * near_w + far_o * far_w
        lower = total[:, HD:] * near_w + far_w
        o_ref[lo:hi, :] = (upper / lower).astype(jnp.bfloat16)


def near_attention(receives, q, kv, far, heads):
    return pl.pallas_call(
        near_kernel,
        out_shape=jax.ShapeDtypeStruct((C, heads * HD), jnp.bfloat16),
        grid_spec=pltpu.PrefetchScalarGridSpec(
            num_scalar_prefetch=1,
            grid=(heads,),
            in_specs=[
                pl.BlockSpec((C, HD), lambda h, *_: (0, h)),
                pl.BlockSpec((C, HD), lambda h, *_: (0, h)),
                pl.BlockSpec((C, HD), lambda h, *_: (0, heads + h)),
                pl.BlockSpec((C + TAIL, HD), lambda h, *_: (0, h)),
            ],
            out_specs=pl.BlockSpec((C, HD), lambda h, *_: (0, h)),
            scratch_shapes=[pltpu.VMEM((C, 2 * HD), jnp.bfloat16)],
        ),
        name="near_attention",
    )(receives, q, kv, kv, far)


def layer(queries, keys, values, pattern):
    groups = lax.axis_size("head")
    spans = lax.axis_size("ctx")
    position = lax.axis_index("ctx")
    far = spans // 2
    tok_rows, width = queries.shape
    heads = H // groups // CHUNKS
    cols = heads * HD
    there = [(c, (c - far) % spans) for c in range(far - 1, spans)]
    back = [(b, a) for a, b in there]
    helpers = sorted(b for _, b in there)
    from_before = [(b - 1, b) for b in helpers if b - 1 in range(far)]
    from_after = [((b + 1) % spans, b) for b in helpers]
    receives = (position >= far - 1).astype(jnp.int32)[None]
    active = ((position < far) | (position == spans - 1)).astype(jnp.int32)[None]

    distances = jnp.array([far - 1, far, far + 1], jnp.int32)
    flags = jnp.where(position >= distances[:, None, None], pattern[:, 0], 0)
    flags = lax.ppermute(flags, "ctx", there)
    lines = jnp.where(flags.transpose(1, 0, 2).reshape(QB, 3 * QB) == 1, 0.0, NEG)
    bias = jnp.repeat(jnp.pad(lines, ((0, 2), (0, 0))), BLOCK, axis=1)

    whole = None
    for n in range(CHUNKS):
        packed = pack((queries, keys, values), groups, cols, n)
        packed = lax.all_to_all(packed, "head", split_axis=0, concat_axis=0, tiled=True)
        packed = packed.reshape(C, 3 * cols)
        q, kv = packed[:, :cols], packed[:, cols:]
        far_q = lax.ppermute(q, "ctx", there)
        before = lax.ppermute(kv, "ctx", from_before)
        after = lax.ppermute(kv, "ctx", from_after)
        far_o = far_attention(active, far_q, kv, before, after, bias, heads)
        far_o = lax.ppermute(far_o, "ctx", back)
        out = near_attention(receives, q, kv, far_o, heads)
        out = lax.all_to_all(
            out.reshape(groups, tok_rows, cols), "head", split_axis=0, concat_axis=0, tiled=True
        )
        whole = unpack(out, whole, width, n)
    return whole


def solution(mesh):
    placed = (
        P(("ctx", "head"), None),
        P(("ctx", "head"), None),
        P(("ctx", "head"), None),
        P(None, "ctx", None, None),
    )
    return jax.shard_map(
        layer, mesh=mesh, in_specs=placed, out_specs=P(("ctx", "head"), None), check_vma=False
    )
```

```python
import functools
import math

import jax
import jax.numpy as jnp
from jax import lax
from jax.experimental import pallas as pl
from jax.experimental.pallas import tpu as pltpu
from jax.sharding import PartitionSpec as P


H = 64
HD = 128
BLOCK = 128
C = 768
QB = C // BLOCK
CHUNKS = 4
ROWS = 256
STEPS = C // ROWS
TAIL = 24
NEG = -1e30
FACTOR = HD**-0.5 * math.log2(math.e)


def eye():
    return lax.broadcasted_iota(jnp.int32, (BLOCK, BLOCK), 0) == lax.broadcasted_iota(
        jnp.int32, (BLOCK, BLOCK), 1
    )


def dot_t(a, b):
    return lax.dot_general(a, b, (((1,), (1,)), ((), ())), preferred_element_type=jnp.float32)


def far_kernel(active, q_ref, ka_ref, kb_ref, kc_ref, bias_ref, o_ref, vx_ref, lse_ref):
    step = pl.program_id(0)
    heads = q_ref.shape[1] // HD
    spans = (ka_ref, kb_ref, kc_ref)

    @pl.when(active[0] > 0)
    def _():
        @pl.when(step == 0)
        def _():
            for h in range(heads):
                for i, kv_ref in enumerate(spans):
                    vx_ref[h, i, :, :HD] = kv_ref[:, (heads + h) * HD : (heads + h + 1) * HD]
                    vx_ref[h, i, :, HD:] = jnp.ones((C, HD), jnp.bfloat16)
            lse_ref[...] = jnp.zeros_like(lse_ref)

        start = pl.multiple_of(step * ROWS, ROWS)
        for h in range(heads):
            own = slice(h * HD, (h + 1) * HD)
            q = q_ref[:, own]
            scores = []
            for i, kv_ref in enumerate(spans):
                raw = dot_t(q, kv_ref[:, own]) * FACTOR
                parts = [
                    raw[r * BLOCK : (r + 1) * BLOCK]
                    + bias_ref[pl.ds(step * (ROWS // BLOCK) + r, 1), i * C : (i + 1) * C]
                    for r in range(ROWS // BLOCK)
                ]
                scores.append(jnp.concatenate(parts, 0))
            top = functools.reduce(
                jnp.maximum, [jnp.max(s, axis=1, keepdims=True) for s in scores]
            )
            total = jnp.zeros((ROWS, 2 * HD), jnp.float32)
            for i, s in enumerate(scores):
                p = jnp.exp2(s - top).astype(jnp.bfloat16)
                total = total + jnp.dot(p, vx_ref[h, i], preferred_element_type=jnp.float32)
            sums = total[:, HD:]
            o_ref[pl.ds(start, ROWS), own] = (total[:, :HD] / sums).astype(jnp.bfloat16)
            lse = top + jnp.log2(sums)
            for r in range(ROWS // BLOCK):
                line = jnp.sum(
                    jnp.where(eye(), lse[r * BLOCK : (r + 1) * BLOCK], 0.0), axis=0, keepdims=True
                )
                lse_ref[h, pl.ds(step * (ROWS // BLOCK) + r, 1), :] = line

        @pl.when(step == STEPS - 1)
        def _():
            for h in range(heads):
                rest = lse_ref[h]
                terms = []
                for _ in range(3):
                    term = rest.astype(jnp.bfloat16).astype(jnp.float32)
                    terms.append(term)
                    rest = rest - term
                o_ref[C:, h * HD : (h + 1) * HD] = jnp.concatenate(terms, 0).astype(jnp.bfloat16)


def pack_kernel(cols, *refs):
    sources, chunks = refs[:3], refs[3:]
    for n, chunk in enumerate(chunks):
        for i, source in enumerate(sources):
            chunk[0, :, i * cols : (i + 1) * cols] = source[:, n * cols : (n + 1) * cols]


def pack(sources, groups, cols):
    rows, width = sources[0].shape
    return pl.pallas_call(
        functools.partial(pack_kernel, cols),
        out_shape=[jax.ShapeDtypeStruct((groups, rows, 3 * cols), jnp.bfloat16)] * CHUNKS,
        grid=(groups,),
        in_specs=[pl.BlockSpec((rows, width // groups), lambda g: (0, g))] * 3,
        out_specs=[pl.BlockSpec((1, rows, 3 * cols), lambda g: (g, 0, 0))] * CHUNKS,
        name="pack",
    )(*sources)


def unpack_kernel(*refs):
    pieces, whole = refs[:-1], refs[-1]
    cols = pieces[0].shape[2]
    for n, piece in enumerate(pieces):
        whole[:, n * cols : (n + 1) * cols] = piece[0]


def unpack(pieces, width):
    groups, rows, cols = pieces[0].shape
    return pl.pallas_call(
        unpack_kernel,
        out_shape=jax.ShapeDtypeStruct((rows, width), jnp.bfloat16),
        grid=(groups,),
        in_specs=[pl.BlockSpec((1, rows, cols), lambda g: (g, 0, 0))] * len(pieces),
        out_specs=pl.BlockSpec((rows, width // groups), lambda g: (0, g)),
        name="unpack",
    )(*pieces)


def far_attention(active, far_q, own, before, after, bias):
    cols = far_q.shape[1]
    heads = cols // HD
    kv = pl.BlockSpec((C, 2 * cols), lambda s, *_: (0, 0))
    return pl.pallas_call(
        far_kernel,
        out_shape=jax.ShapeDtypeStruct((C + TAIL, cols), jnp.bfloat16),
        grid_spec=pltpu.PrefetchScalarGridSpec(
            num_scalar_prefetch=1,
            grid=(STEPS,),
            in_specs=[
                pl.BlockSpec((ROWS, cols), lambda s, *_: (s, 0)),
                kv, kv, kv,
                pl.BlockSpec((8, 3 * C), lambda s, *_: (0, 0)),
            ],
            out_specs=pl.BlockSpec((C + TAIL, cols), lambda s, *_: (0, 0)),
            scratch_shapes=[
                pltpu.VMEM((heads, 3, C, 2 * HD), jnp.bfloat16),
                pltpu.VMEM((heads, 8, BLOCK), jnp.float32),
            ],
        ),
        name="far_attention",
    )(active, far_q, after, own, before, bias)


def near_kernel(receives, q_ref, kv_ref, far_ref, o_ref, vx_ref):
    heads = q_ref.shape[1] // HD
    for h in range(heads):
        own = slice(h * HD, (h + 1) * HD)
        vx_ref[h, :, :HD] = kv_ref[:, (heads + h) * HD : (heads + h + 1) * HD]
        vx_ref[h, :, HD:] = jnp.ones((C, HD), jnp.bfloat16)
        tail = far_ref[C:, own].astype(jnp.float32)
        lse_all = tail[0:8] + (tail[8:16] + tail[16:24])
        lse_all = jnp.where(receives[0] > 0, lse_all, NEG)
        for step in range(STEPS):
            lo, hi = step * ROWS, (step + 1) * ROWS
            s = dot_t(q_ref[lo:hi, own], kv_ref[:hi, own]) * FACTOR
            rows = lo + lax.broadcasted_iota(jnp.int32, (ROWS, hi), 0)
            cols = lax.broadcasted_iota(jnp.int32, (ROWS, hi), 1)
            s = jnp.where(rows >= cols, s, NEG)
            top = jnp.max(s, axis=1, keepdims=True)
            p = jnp.exp2(s - top).astype(jnp.bfloat16)
            total = jnp.dot(p, vx_ref[h, :hi, :], preferred_element_type=jnp.float32)
            columns = []
            for r in range(ROWS // BLOCK):
                line = lse_all[step * (ROWS // BLOCK) + r][None, :]
                columns.append(jnp.sum(jnp.where(eye(), line, 0.0), axis=1, keepdims=True))
            far_lse = jnp.concatenate(columns, 0)
            peak = jnp.maximum(top, far_lse)
            near_w = jnp.exp2(top - peak)
            far_w = jnp.exp2(far_lse - peak)
            far_o = far_ref[lo:hi, own].astype(jnp.float32)
            upper = total[:, :HD] * near_w + far_o * far_w
            lower = total[:, HD:] * near_w + far_w
            o_ref[lo:hi, own] = (upper / lower).astype(jnp.bfloat16)


def near_attention(receives, q, kv, far):
    cols = q.shape[1]

    def full(a):
        return pl.BlockSpec(a.shape, lambda i, *_: (0, 0))

    return pl.pallas_call(
        near_kernel,
        out_shape=jax.ShapeDtypeStruct(q.shape, jnp.bfloat16),
        grid_spec=pltpu.PrefetchScalarGridSpec(
            num_scalar_prefetch=1,
            grid=(1,),
            in_specs=[full(q), full(kv), full(far)],
            out_specs=full(q),
            scratch_shapes=[pltpu.VMEM((cols // HD, C, 2 * HD), jnp.bfloat16)],
        ),
        name="near_attention",
    )(receives, q, kv, far)


def layer(queries, keys, values, pattern):
    groups = lax.axis_size("head")
    spans = lax.axis_size("ctx")
    position = lax.axis_index("ctx")
    far = spans // 2
    tok_rows, width = queries.shape
    cols = H // groups // CHUNKS * HD
    there = [(c, (c - far) % spans) for c in range(far - 1, spans)]
    back = [(b, a) for a, b in there]
    helpers = sorted(b for _, b in there)
    from_before = [(b - 1, b) for b in helpers if b - 1 in range(far)]
    from_after = [((b + 1) % spans, b) for b in helpers]
    receives = (position >= far - 1).astype(jnp.int32)[None]
    active = ((position < far) | (position == spans - 1)).astype(jnp.int32)[None]

    distances = jnp.array([far - 1, far, far + 1], jnp.int32)
    flags = jnp.where(position >= distances[:, None, None], pattern[:, 0], 0)
    flags = lax.ppermute(flags, "ctx", there)
    lines = jnp.where(flags.transpose(1, 0, 2).reshape(QB, 3 * QB) == 1, 0.0, NEG)
    bias = jnp.repeat(jnp.pad(lines, ((0, 2), (0, 0))), BLOCK, axis=1)

    chunks = pack((queries, keys, values), groups, cols)
    pieces = []
    for packed in chunks:
        packed = lax.all_to_all(packed, "head", split_axis=0, concat_axis=0, tiled=True)
        packed = packed.reshape(C, 3 * cols)
        q, kv = packed[:, :cols], packed[:, cols:]
        far_q = lax.ppermute(q, "ctx", there)
        before = lax.ppermute(kv, "ctx", from_before)
        after = lax.ppermute(kv, "ctx", from_after)
        far_o = far_attention(active, far_q, kv, before, after, bias)
        far_o = lax.ppermute(far_o, "ctx", back)
        out = near_attention(receives, q, kv, far_o)
        out = lax.all_to_all(
            out.reshape(groups, tok_rows, cols), "head", split_axis=0, concat_axis=0, tiled=True
        )
        pieces.append(out)
    return unpack(pieces, width)


def solution(mesh):
    placed = (
        P(("ctx", "head"), None),
        P(("ctx", "head"), None),
        P(("ctx", "head"), None),
        P(None, "ctx", None, None),
    )
    return jax.shard_map(
        layer, mesh=mesh, in_specs=placed, out_specs=P(("ctx", "head"), None), check_vma=False
    )
```

```python
import functools
import math

import jax
import jax.numpy as jnp
from jax import lax
from jax.experimental import pallas as pl
from jax.experimental.pallas import tpu as pltpu
from jax.sharding import PartitionSpec as P


H = 64
HD = 128
BLOCK = 128
C = 768
QB = C // BLOCK
MODES = ("q", "kv", "q", "q")
CHUNKS = len(MODES)
ROWS = 256
STEPS = C // ROWS
TAIL = 24
NEG = -1e30
FACTOR = HD**-0.5 * math.log2(math.e)


def eye():
    return lax.broadcasted_iota(jnp.int32, (BLOCK, BLOCK), 0) == lax.broadcasted_iota(
        jnp.int32, (BLOCK, BLOCK), 1
    )


def dot_t(a, b):
    return lax.dot_general(a, b, (((1,), (1,)), ((), ())), preferred_element_type=jnp.float32)


def far_kernel(active, q_ref, ka_ref, kb_ref, kc_ref, bias_ref, o_ref, vx_ref, lse_ref):
    step = pl.program_id(0)
    heads = q_ref.shape[1] // HD
    spans = (ka_ref, kb_ref, kc_ref)

    @pl.when(active[0] > 0)
    def _():
        @pl.when(step == 0)
        def _():
            for h in range(heads):
                for i, kv_ref in enumerate(spans):
                    vx_ref[h, i, :, :HD] = kv_ref[:, (heads + h) * HD : (heads + h + 1) * HD]
                    vx_ref[h, i, :, HD:] = jnp.ones((C, HD), jnp.bfloat16)
            lse_ref[...] = jnp.zeros_like(lse_ref)

        start = pl.multiple_of(step * ROWS, ROWS)
        for h in range(heads):
            own = slice(h * HD, (h + 1) * HD)
            q = q_ref[:, own]
            scores = []
            for i, kv_ref in enumerate(spans):
                raw = dot_t(q, kv_ref[:, own]) * FACTOR
                parts = [
                    raw[r * BLOCK : (r + 1) * BLOCK]
                    + bias_ref[pl.ds(step * (ROWS // BLOCK) + r, 1), i * C : (i + 1) * C]
                    for r in range(ROWS // BLOCK)
                ]
                scores.append(jnp.concatenate(parts, 0))
            top = functools.reduce(
                jnp.maximum, [jnp.max(s, axis=1, keepdims=True) for s in scores]
            )
            total = jnp.zeros((ROWS, 2 * HD), jnp.float32)
            for i, s in enumerate(scores):
                p = jnp.exp2(s - top).astype(jnp.bfloat16)
                total = total + jnp.dot(p, vx_ref[h, i], preferred_element_type=jnp.float32)
            sums = total[:, HD:]
            o_ref[pl.ds(start, ROWS), own] = (total[:, :HD] / sums).astype(jnp.bfloat16)
            lse = top + jnp.log2(sums)
            for r in range(ROWS // BLOCK):
                line = jnp.sum(
                    jnp.where(eye(), lse[r * BLOCK : (r + 1) * BLOCK], 0.0), axis=0, keepdims=True
                )
                lse_ref[h, pl.ds(step * (ROWS // BLOCK) + r, 1), :] = line

        @pl.when(step == STEPS - 1)
        def _():
            for h in range(heads):
                rest = lse_ref[h]
                terms = []
                for _ in range(3):
                    term = rest.astype(jnp.bfloat16).astype(jnp.float32)
                    terms.append(term)
                    rest = rest - term
                o_ref[C:, h * HD : (h + 1) * HD] = jnp.concatenate(terms, 0).astype(jnp.bfloat16)


def pack_kernel(cols, *refs):
    sources, chunks = refs[:3], refs[3:]
    for n, chunk in enumerate(chunks):
        for i, source in enumerate(sources):
            chunk[0, :, i * cols : (i + 1) * cols] = source[:, n * cols : (n + 1) * cols]


def pack(sources, groups, cols):
    rows, width = sources[0].shape
    return pl.pallas_call(
        functools.partial(pack_kernel, cols),
        out_shape=[jax.ShapeDtypeStruct((groups, rows, 3 * cols), jnp.bfloat16)] * CHUNKS,
        grid=(groups,),
        in_specs=[pl.BlockSpec((rows, width // groups), lambda g: (0, g))] * 3,
        out_specs=[pl.BlockSpec((1, rows, 3 * cols), lambda g: (g, 0, 0))] * CHUNKS,
        name="pack",
    )(*sources)


def unpack_kernel(*refs):
    pieces, whole = refs[:-1], refs[-1]
    cols = pieces[0].shape[2]
    for n, piece in enumerate(pieces):
        whole[:, n * cols : (n + 1) * cols] = piece[0]


def unpack(pieces, width):
    groups, rows, cols = pieces[0].shape
    return pl.pallas_call(
        unpack_kernel,
        out_shape=jax.ShapeDtypeStruct((rows, width), jnp.bfloat16),
        grid=(groups,),
        in_specs=[pl.BlockSpec((1, rows, cols), lambda g: (g, 0, 0))] * len(pieces),
        out_specs=pl.BlockSpec((rows, width // groups), lambda g: (0, g)),
        name="unpack",
    )(*pieces)


def far_attention(active, far_q, own, before, after, bias):
    cols = far_q.shape[1]
    heads = cols // HD
    kv = pl.BlockSpec((C, 2 * cols), lambda s, *_: (0, 0))
    return pl.pallas_call(
        far_kernel,
        out_shape=jax.ShapeDtypeStruct((C + TAIL, cols), jnp.bfloat16),
        grid_spec=pltpu.PrefetchScalarGridSpec(
            num_scalar_prefetch=1,
            grid=(STEPS,),
            in_specs=[
                pl.BlockSpec((ROWS, cols), lambda s, *_: (s, 0)),
                kv, kv, kv,
                pl.BlockSpec((8, 3 * C), lambda s, *_: (0, 0)),
            ],
            out_specs=pl.BlockSpec((C + TAIL, cols), lambda s, *_: (0, 0)),
            scratch_shapes=[
                pltpu.VMEM((heads, 3, C, 2 * HD), jnp.bfloat16),
                pltpu.VMEM((heads, 8, BLOCK), jnp.float32),
            ],
        ),
        name="far_attention",
    )(active, far_q, after, own, before, bias)


def near_kernel(receives, q_ref, kv_ref, far_ref, o_ref, vx_ref):
    heads = q_ref.shape[1] // HD
    for h in range(heads):
        own = slice(h * HD, (h + 1) * HD)
        vx_ref[h, :, :HD] = kv_ref[:, (heads + h) * HD : (heads + h + 1) * HD]
        vx_ref[h, :, HD:] = jnp.ones((C, HD), jnp.bfloat16)
        tail = far_ref[C:, own].astype(jnp.float32)
        lse_all = tail[0:8] + (tail[8:16] + tail[16:24])
        lse_all = jnp.where(receives[0] > 0, lse_all, NEG)
        for step in range(STEPS):
            lo, hi = step * ROWS, (step + 1) * ROWS
            s = dot_t(q_ref[lo:hi, own], kv_ref[:hi, own]) * FACTOR
            rows = lo + lax.broadcasted_iota(jnp.int32, (ROWS, hi), 0)
            cols = lax.broadcasted_iota(jnp.int32, (ROWS, hi), 1)
            s = jnp.where(rows >= cols, s, NEG)
            top = jnp.max(s, axis=1, keepdims=True)
            p = jnp.exp2(s - top).astype(jnp.bfloat16)
            total = jnp.dot(p, vx_ref[h, :hi, :], preferred_element_type=jnp.float32)
            columns = []
            for r in range(ROWS // BLOCK):
                line = lse_all[step * (ROWS // BLOCK) + r][None, :]
                columns.append(jnp.sum(jnp.where(eye(), line, 0.0), axis=1, keepdims=True))
            far_lse = jnp.concatenate(columns, 0)
            peak = jnp.maximum(top, far_lse)
            near_w = jnp.exp2(top - peak)
            far_w = jnp.exp2(far_lse - peak)
            far_o = jnp.where(receives[0] > 0, far_ref[lo:hi, own].astype(jnp.float32), 0.0)
            upper = total[:, :HD] * near_w + far_o * far_w
            lower = total[:, HD:] * near_w + far_w
            o_ref[lo:hi, own] = (upper / lower).astype(jnp.bfloat16)


def near_attention(receives, q, kv, far):
    cols = q.shape[1]

    def full(a):
        return pl.BlockSpec(a.shape, lambda i, *_: (0, 0))

    return pl.pallas_call(
        near_kernel,
        out_shape=jax.ShapeDtypeStruct(q.shape, jnp.bfloat16),
        grid_spec=pltpu.PrefetchScalarGridSpec(
            num_scalar_prefetch=1,
            grid=(1,),
            in_specs=[full(q), full(kv), full(far)],
            out_specs=full(q),
            scratch_shapes=[pltpu.VMEM((cols // HD, C, 2 * HD), jnp.bfloat16)],
        ),
        name="near_attention",
    )(receives, q, kv, far)


def layer(queries, keys, values, pattern):
    groups = lax.axis_size("head")
    spans = lax.axis_size("ctx")
    position = lax.axis_index("ctx")
    far = spans // 2
    tok_rows, width = queries.shape
    cols = H // groups // CHUNKS * HD
    there = [(c, (c - far) % spans) for c in range(far - 1, spans)]
    back = [(b, a) for a, b in there]
    helpers = sorted(b for _, b in there)
    from_before = [(b - 1, b) for b in helpers if b - 1 in range(far)]
    from_after = [((b + 1) % spans, b) for b in helpers]
    ahead = [(s, (s + far) % spans) for s in range(far + 1)]
    readers = range(far - 1, spans)
    pass_before = [(c - 1, c) for c in readers if c > far]
    pass_after = [((c + 1) % spans, c) for c in readers]
    reads_far = position >= far - 1
    receives = reads_far.astype(jnp.int32)[None]
    active = ((position < far) | (position == spans - 1)).astype(jnp.int32)[None]

    distances = jnp.array([far - 1, far, far + 1], jnp.int32)
    flags = jnp.where(position >= distances[:, None, None], pattern[:, 0], 0)

    def bias_of(flags):
        lines = jnp.where(flags.transpose(1, 0, 2).reshape(QB, 3 * QB) == 1, 0.0, NEG)
        return jnp.repeat(jnp.pad(lines, ((0, 2), (0, 0))), BLOCK, axis=1)

    own_bias = bias_of(flags)
    bias = bias_of(lax.ppermute(flags, "ctx", there))

    chunks = pack((queries, keys, values), groups, cols)
    pieces = []
    for n, packed in enumerate(chunks):
        packed = lax.all_to_all(packed, "head", split_axis=0, concat_axis=0, tiled=True)
        packed = packed.reshape(C, 3 * cols)
        q, kv = packed[:, :cols], packed[:, cols:]
        if MODES[n] == "kv":
            shipped = lax.ppermute(kv, "ctx", ahead)
            before = lax.ppermute(shipped, "ctx", pass_before)
            after = lax.ppermute(shipped, "ctx", pass_after)
            far_o = far_attention(receives, q, shipped, before, after, own_bias)
        else:
            far_q = lax.ppermute(q, "ctx", there)
            before = lax.ppermute(kv, "ctx", from_before)
            after = lax.ppermute(kv, "ctx", from_after)
            far_o = far_attention(active, far_q, kv, before, after, bias)
            far_o = lax.ppermute(far_o, "ctx", back)
        out = near_attention(receives, q, kv, far_o)
        out = lax.all_to_all(
            out.reshape(groups, tok_rows, cols), "head", split_axis=0, concat_axis=0, tiled=True
        )
        pieces.append(out)
    return unpack(pieces, width)


def solution(mesh):
    placed = (
        P(("ctx", "head"), None),
        P(("ctx", "head"), None),
        P(("ctx", "head"), None),
        P(None, "ctx", None, None),
    )
    return jax.shard_map(
        layer, mesh=mesh, in_specs=placed, out_specs=P(("ctx", "head"), None), check_vma=False
    )
```

```python
import functools
import math

import jax
import jax.numpy as jnp
from jax import lax
from jax.experimental import pallas as pl
from jax.experimental.pallas import tpu as pltpu
from jax.sharding import PartitionSpec as P


H = 64
HD = 128
BLOCK = 128
C = 768
QB = C // BLOCK
MODES = ("q", "kv", "q", "q")
CHUNKS = len(MODES)
ROWS = 256
STEPS = C // ROWS
TAIL = 24
NEG = -1e30
FACTOR = HD**-0.5 * math.log2(math.e)


def eye():
    return lax.broadcasted_iota(jnp.int32, (BLOCK, BLOCK), 0) == lax.broadcasted_iota(
        jnp.int32, (BLOCK, BLOCK), 1
    )


def dot_t(a, b):
    return lax.dot_general(a, b, (((1,), (1,)), ((), ())), preferred_element_type=jnp.float32)


def far_kernel(active, q_ref, ka_ref, kb_ref, kc_ref, bias_ref, o_ref, vx_ref, lse_ref):
    step = pl.program_id(0)
    heads = q_ref.shape[1] // HD
    spans = (ka_ref, kb_ref, kc_ref)

    @pl.when(active[0] > 0)
    def _():
        @pl.when(step == 0)
        def _():
            for h in range(heads):
                for i, kv_ref in enumerate(spans):
                    vx_ref[h, i, :, :HD] = kv_ref[:, (heads + h) * HD : (heads + h + 1) * HD]
                    vx_ref[h, i, :, HD:] = jnp.ones((C, HD), jnp.bfloat16)
            lse_ref[...] = jnp.zeros_like(lse_ref)

        start = pl.multiple_of(step * ROWS, ROWS)
        for h in range(heads):
            own = slice(h * HD, (h + 1) * HD)
            q = q_ref[:, own]
            scores = []
            for i, kv_ref in enumerate(spans):
                raw = dot_t(q, kv_ref[:, own]) * FACTOR
                parts = [
                    raw[r * BLOCK : (r + 1) * BLOCK]
                    + bias_ref[pl.ds(step * (ROWS // BLOCK) + r, 1), i * C : (i + 1) * C]
                    for r in range(ROWS // BLOCK)
                ]
                scores.append(jnp.concatenate(parts, 0))
            top = functools.reduce(
                jnp.maximum, [jnp.max(s, axis=1, keepdims=True) for s in scores]
            )
            total = jnp.zeros((ROWS, 2 * HD), jnp.float32)
            for i, s in enumerate(scores):
                p = jnp.exp2(s - top).astype(jnp.bfloat16)
                total = total + jnp.dot(p, vx_ref[h, i], preferred_element_type=jnp.float32)
            sums = total[:, HD:]
            o_ref[pl.ds(start, ROWS), own] = (total[:, :HD] / sums).astype(jnp.bfloat16)
            lse = top + jnp.log2(sums)
            for r in range(ROWS // BLOCK):
                line = jnp.sum(
                    jnp.where(eye(), lse[r * BLOCK : (r + 1) * BLOCK], 0.0), axis=0, keepdims=True
                )
                lse_ref[h, pl.ds(step * (ROWS // BLOCK) + r, 1), :] = line

        @pl.when(step == STEPS - 1)
        def _():
            for h in range(heads):
                rest = lse_ref[h]
                terms = []
                for _ in range(3):
                    term = rest.astype(jnp.bfloat16).astype(jnp.float32)
                    terms.append(term)
                    rest = rest - term
                o_ref[C:, h * HD : (h + 1) * HD] = jnp.concatenate(terms, 0).astype(jnp.bfloat16)


def pack_kernel(cols, *refs):
    sources, chunks = refs[:3], refs[3:]
    for n, chunk in enumerate(chunks):
        for i, source in enumerate(sources):
            chunk[0, :, i * cols : (i + 1) * cols] = source[:, n * cols : (n + 1) * cols]


def pack(sources, groups, cols):
    rows, width = sources[0].shape
    return pl.pallas_call(
        functools.partial(pack_kernel, cols),
        out_shape=[jax.ShapeDtypeStruct((groups, rows, 3 * cols), jnp.bfloat16)] * CHUNKS,
        grid=(groups,),
        in_specs=[pl.BlockSpec((rows, width // groups), lambda g: (0, g))] * 3,
        out_specs=[pl.BlockSpec((1, rows, 3 * cols), lambda g: (g, 0, 0))] * CHUNKS,
        name="pack",
    )(*sources)


def unpack_kernel(*refs):
    pieces, whole = refs[:-1], refs[-1]
    groups, _, cols = pieces[0].shape
    for g in range(groups):
        for n, piece in enumerate(pieces):
            start = (g * len(pieces) + n) * cols
            whole[:, start : start + cols] = piece[g]


def unpack(pieces, width):
    groups, rows, cols = pieces[0].shape
    steps = 2
    return pl.pallas_call(
        unpack_kernel,
        out_shape=jax.ShapeDtypeStruct((rows, width), jnp.bfloat16),
        grid=(steps,),
        in_specs=[pl.BlockSpec((groups // steps, rows, cols), lambda g: (g, 0, 0))] * len(pieces),
        out_specs=pl.BlockSpec((rows, width // steps), lambda g: (0, g)),
        name="unpack",
    )(*pieces)


def far_attention(active, far_q, own, before, after, bias):
    cols = far_q.shape[1]
    heads = cols // HD
    kv = pl.BlockSpec((C, 2 * cols), lambda s, *_: (0, 0))
    return pl.pallas_call(
        far_kernel,
        out_shape=jax.ShapeDtypeStruct((C + TAIL, cols), jnp.bfloat16),
        grid_spec=pltpu.PrefetchScalarGridSpec(
            num_scalar_prefetch=1,
            grid=(STEPS,),
            in_specs=[
                pl.BlockSpec((ROWS, cols), lambda s, *_: (s, 0)),
                kv, kv, kv,
                pl.BlockSpec((8, 3 * C), lambda s, *_: (0, 0)),
            ],
            out_specs=pl.BlockSpec((C + TAIL, cols), lambda s, *_: (0, 0)),
            scratch_shapes=[
                pltpu.VMEM((heads, 3, C, 2 * HD), jnp.bfloat16),
                pltpu.VMEM((heads, 8, BLOCK), jnp.float32),
            ],
        ),
        name="far_attention",
    )(active, far_q, after, own, before, bias)


def near_kernel(receives, q_ref, kv_ref, far_ref, o_ref, vx_ref):
    heads = q_ref.shape[1] // HD
    for h in range(heads):
        own = slice(h * HD, (h + 1) * HD)
        vx_ref[h, :, :HD] = kv_ref[:, (heads + h) * HD : (heads + h + 1) * HD]
        vx_ref[h, :, HD:] = jnp.ones((C, HD), jnp.bfloat16)
        tail = far_ref[C:, own].astype(jnp.float32)
        lse_all = tail[0:8] + (tail[8:16] + tail[16:24])
        lse_all = jnp.where(receives[0] > 0, lse_all, NEG)
        for step in range(STEPS):
            lo, hi = step * ROWS, (step + 1) * ROWS
            s = dot_t(q_ref[lo:hi, own], kv_ref[:hi, own]) * FACTOR
            rows = lo + lax.broadcasted_iota(jnp.int32, (ROWS, hi), 0)
            cols = lax.broadcasted_iota(jnp.int32, (ROWS, hi), 1)
            s = jnp.where(rows >= cols, s, NEG)
            top = jnp.max(s, axis=1, keepdims=True)
            p = jnp.exp2(s - top).astype(jnp.bfloat16)
            total = jnp.dot(p, vx_ref[h, :hi, :], preferred_element_type=jnp.float32)
            columns = []
            for r in range(ROWS // BLOCK):
                line = lse_all[step * (ROWS // BLOCK) + r][None, :]
                columns.append(jnp.sum(jnp.where(eye(), line, 0.0), axis=1, keepdims=True))
            far_lse = jnp.concatenate(columns, 0)
            peak = jnp.maximum(top, far_lse)
            near_w = jnp.exp2(top - peak)
            far_w = jnp.exp2(far_lse - peak)
            far_o = jnp.where(receives[0] > 0, far_ref[lo:hi, own].astype(jnp.float32), 0.0)
            upper = total[:, :HD] * near_w + far_o * far_w
            lower = total[:, HD:] * near_w + far_w
            o_ref[lo:hi, own] = (upper / lower).astype(jnp.bfloat16)


def near_attention(receives, q, kv, far):
    cols = q.shape[1]

    def full(a):
        return pl.BlockSpec(a.shape, lambda i, *_: (0, 0))

    return pl.pallas_call(
        near_kernel,
        out_shape=jax.ShapeDtypeStruct(q.shape, jnp.bfloat16),
        grid_spec=pltpu.PrefetchScalarGridSpec(
            num_scalar_prefetch=1,
            grid=(1,),
            in_specs=[full(q), full(kv), full(far)],
            out_specs=full(q),
            scratch_shapes=[pltpu.VMEM((cols // HD, C, 2 * HD), jnp.bfloat16)],
        ),
        name="near_attention",
    )(receives, q, kv, far)


def layer(queries, keys, values, pattern):
    groups = lax.axis_size("head")
    spans = lax.axis_size("ctx")
    position = lax.axis_index("ctx")
    far = spans // 2
    tok_rows, width = queries.shape
    cols = H // groups // CHUNKS * HD
    there = [(c, (c - far) % spans) for c in range(far - 1, spans)]
    back = [(b, a) for a, b in there]
    helpers = sorted(b for _, b in there)
    from_before = [(b - 1, b) for b in helpers if b - 1 in range(far)]
    from_after = [((b + 1) % spans, b) for b in helpers]
    ahead = [(s, (s + far) % spans) for s in range(far + 1)]
    readers = range(far - 1, spans)
    pass_before = [(c - 1, c) for c in readers if c > far]
    pass_after = [((c + 1) % spans, c) for c in readers]
    reads_far = position >= far - 1
    receives = reads_far.astype(jnp.int32)[None]
    active = ((position < far) | (position == spans - 1)).astype(jnp.int32)[None]

    distances = jnp.array([far - 1, far, far + 1], jnp.int32)
    flags = jnp.where(position >= distances[:, None, None], pattern[:, 0], 0)

    def bias_of(flags):
        lines = jnp.where(flags.transpose(1, 0, 2).reshape(QB, 3 * QB) == 1, 0.0, NEG)
        return jnp.repeat(jnp.pad(lines, ((0, 2), (0, 0))), BLOCK, axis=1)

    own_bias = bias_of(flags)
    bias = bias_of(lax.ppermute(flags, "ctx", there))

    chunks = pack((queries, keys, values), groups, cols)
    pieces = []
    for n, packed in enumerate(chunks):
        packed = lax.all_to_all(packed, "head", split_axis=0, concat_axis=0, tiled=True)
        packed = packed.reshape(C, 3 * cols)
        q, kv = packed[:, :cols], packed[:, cols:]
        if MODES[n] == "kv":
            shipped = lax.ppermute(kv, "ctx", ahead)
            before = lax.ppermute(shipped, "ctx", pass_before)
            after = lax.ppermute(shipped, "ctx", pass_after)
            far_o = far_attention(receives, q, shipped, before, after, own_bias)
        else:
            far_q = lax.ppermute(q, "ctx", there)
            before = lax.ppermute(kv, "ctx", from_before)
            after = lax.ppermute(kv, "ctx", from_after)
            far_o = far_attention(active, far_q, kv, before, after, bias)
            far_o = lax.ppermute(far_o, "ctx", back)
        out = near_attention(receives, q, kv, far_o)
        out = lax.all_to_all(
            out.reshape(groups, tok_rows, cols), "head", split_axis=0, concat_axis=0, tiled=True
        )
        pieces.append(out)
    return unpack(pieces, width)


def solution(mesh):
    placed = (
        P(("ctx", "head"), None),
        P(("ctx", "head"), None),
        P(("ctx", "head"), None),
        P(None, "ctx", None, None),
    )
    return jax.shard_map(
        layer, mesh=mesh, in_specs=placed, out_specs=P(("ctx", "head"), None), check_vma=False
    )
```
